512 devices in a mesh: dp: 16 (over z, core), seq: 32 (over x, y).
Axes of the slice: x: 4, y: 8, z: 8, core: 2. Of those that a mesh axis runs over, the one named last changes fastest.
Arguments:
- inputs: bfloat16 [16, 4096, 1024], P('dp', 'seq'), may hold values from -6 to 6
- cotangent: bfloat16 [16, 4096, 512], P('dp', 'seq'), may hold values from -6 to 6
- qkv_weight: bfloat16 [1024, 1536], P('seq'), may hold values from -0.1875 to 0.1875
Outputs:
- output: bfloat16 [16, 4096, 512], P('dp', 'seq')
- input_grad: bfloat16 [16, 4096, 1024], P('dp', 'seq')
- weight_grad: float32 [1024, 1536], P('seq')
The draws below stay inside these ranges and needn't reach their ends.
All inputs are finite; a program needn't handle non-finite values.
Results may differ from the reference program's by a relative error of at most 0.023.
Values may be sent and summed in bfloat16 or wider, within the bound.
A program may use at most 64 MiB of HBM per device.

```python
import jax
import jax.numpy as jnp
from jax import lax

D = 1024
HEADS = 4
DH = 128
BLOCK = 128
TOK_DEV = 128
HD = 512
LENGTH = 4096
BATCH = 16
N_SEQ = 32


def with_spikes(array, key, source, target, blocks, factor):
    owner, partner = [(jnp.arange(array.shape[position]) // (array.shape[position] // blocks)).reshape([-1 if axis == position else 1 for axis in range(array.ndim)]) for position in (source, target)]
    chosen = jax.random.permutation(key, blocks)[partner]
    strong = (owner == chosen) | (owner == (partner + blocks // 2) % blocks)
    return jnp.where(strong, factor * array, array)


def levels(rng, shape, pieces, low, top_value):
    def one(axis_at, blocks):
        steps = jax.random.uniform(jax.random.fold_in(jax.random.fold_in(rng, 6), axis_at), (blocks,), jnp.float32, low / len(pieces), top_value / len(pieces))
        return jnp.repeat(jnp.exp(steps), shape[axis_at] // blocks).reshape((-1,) + (1,) * (len(shape) - axis_at - 1))

    level = one(*pieces[0])
    for cut in pieces[1:]:
        level = level * one(*cut)
    return level


def bell_draw(stream_key, shape, scale, most, cuts=(), dtype=jnp.bfloat16):
    factor_of = levels(stream_key, shape, cuts, -0.22, 0.18) if cuts else 1.0
    array = jax.random.normal(stream_key, shape, jnp.float32) * scale * factor_of
    return jnp.minimum(jnp.maximum(array, -most), most).astype(dtype)


def gaussian_with(key, dims, scale, limit, cuts, heavy, held_as=jnp.bfloat16):
    values = scale * jax.random.normal(key, dims, jnp.float32)
    if cuts:
        values = values * levels(key, dims, cuts, -0.22, 0.18)
    return jnp.clip(with_spikes(values, jax.random.fold_in(key, 3), *heavy), -limit, limit).astype(held_as)


def setup_inputs(seed: int = 0) -> dict:
    key_of = jax.random.split(jax.random.key(seed), 4)
    return {
        "inputs": gaussian_with(key_of[0], (BATCH, LENGTH, D), 1.0, 6.0, ((0, 16), (1, 32)), (1, 2, 32, 2.75)),
        "cotangent": bell_draw(key_of[1], (BATCH, LENGTH, HD), 1.0, 6.0, ((0, 16), (1, 32))),
        "qkv_weight": bell_draw(key_of[2], (D, 3 * HD), D ** -0.5, 0.1875, ((0, 32),)),
    }


EPS = 1e-05
HIGH = lax.Precision.HIGHEST

def rms_scale(field):
    return field * lax.rsqrt(lax.optimization_barrier(jnp.mean(field * field, axis=-1, keepdims=True)) + EPS)

def causal_table(width):
    row_index = lax.broadcasted_iota(jnp.int32, (width, width), 0)
    col_index = lax.broadcasted_iota(jnp.int32, (width, width), 1)
    return row_index >= col_index

def exclusive_sum(terms):
    running = jnp.cumsum(terms, axis=0)
    return jnp.concatenate([jnp.zeros_like(terms[:1]), running[:-1]], axis=0)

def suffix_sum(terms):
    running = jnp.cumsum(terms[::-1], axis=0)[::-1]
    return jnp.concatenate([running[1:], jnp.zeros_like(terms[:1])], axis=0)

def one_sequence(inputs, cotangent, qkv_weight):
    width = HEADS * DH
    count = LENGTH // BLOCK
    proj = jnp.dot(inputs, qkv_weight, preferred_element_type=jnp.float32).astype(jnp.bfloat16)

    def split(block_data):
        return block_data.reshape(count, BLOCK, HEADS, DH).astype(jnp.float32)
    query_rows = split(proj[:, :width])
    key_rows = split(proj[:, width:2 * width])
    value_rows = split(proj[:, 2 * width:])
    local_states = jnp.einsum('cbhi,cbhj->chij', key_rows, value_rows, precision=HIGH)
    states = exclusive_sum(local_states)
    causal = causal_table(BLOCK)
    scores = jnp.einsum('cbhi,cehi->chbe', query_rows, key_rows, precision=HIGH)
    score_weights = jnp.where(causal, scores, 0.0).astype(jnp.bfloat16).astype(jnp.float32)
    mixed = jnp.einsum('chbe,cehj->cbhj', score_weights, value_rows, precision=HIGH)
    mixed = mixed + jnp.einsum('cbhi,chij->cbhj', query_rows, states, precision=HIGH)
    output = rms_scale(mixed).astype(jnp.bfloat16)
    upstream = cotangent.reshape(count, BLOCK, HEADS, DH).astype(jnp.float32)
    unused, pullback = jax.vjp(rms_scale, mixed)
    grad_mixed = pullback(upstream)[0].astype(jnp.bfloat16).astype(jnp.float32)
    local_cot = jnp.einsum('cbhi,cbhj->chij', query_rows, grad_mixed, precision=HIGH)
    suffixes = suffix_sum(local_cot)
    back_scores = jnp.einsum('cbhj,cehj->chbe', grad_mixed, value_rows, precision=HIGH)
    back_weights = jnp.where(causal, back_scores, 0.0).astype(jnp.bfloat16).astype(jnp.float32)
    grad_query = jnp.einsum('chbe,cehi->cbhi', back_weights, key_rows, precision=HIGH)
    grad_query = grad_query + jnp.einsum('cbhj,chij->cbhi', grad_mixed, states, precision=HIGH)
    grad_key = jnp.einsum('chbe,cbhi->cehi', back_weights, query_rows, precision=HIGH)
    grad_key = grad_key + jnp.einsum('cehj,chij->cehi', value_rows, suffixes, precision=HIGH)
    grad_value = jnp.einsum('chbe,cbhj->cehj', score_weights, grad_mixed, precision=HIGH)
    grad_value = grad_value + jnp.einsum('cehi,chij->cehj', key_rows, suffixes, precision=HIGH)
    grads = jnp.concatenate([grad_query.reshape(LENGTH, width), grad_key.reshape(LENGTH, width), grad_value.reshape(LENGTH, width)], axis=1).astype(jnp.bfloat16)
    input_grad = jnp.dot(grads, qkv_weight.T, preferred_element_type=jnp.float32).astype(jnp.bfloat16)
    range_inputs = inputs.reshape(N_SEQ, TOK_DEV, D).astype(jnp.float32)
    range_grads = grads.reshape(N_SEQ, TOK_DEV, 3 * width).astype(jnp.float32)
    partial_value = jnp.einsum('snd,snk->sdk', range_inputs, range_grads, precision=HIGH).astype(jnp.bfloat16)
    partial_value = lax.optimization_barrier(partial_value)
    weight_part = lax.optimization_barrier(jnp.sum(partial_value.astype(jnp.float32), axis=0))
    return (output.reshape(LENGTH, width), input_grad, weight_part)

def reference(inputs, cotangent, qkv_weight):

    def run(pair):
        return one_sequence(pair[0], pair[1], qkv_weight)
    output, input_grad, weight_parts = lax.map(run, (inputs, cotangent))
    return (output, input_grad, lax.optimization_barrier(jnp.sum(weight_parts, axis=0)))
```

```python
import jax
import jax.numpy as jnp
from jax import lax
from jax.experimental import pallas as pl
from jax.experimental.pallas import tpu as pltpu
from jax.sharding import PartitionSpec as P

HEADS, DH, TOK = 4, 128, 128
D, HD = 1024, 512
NX, NY, NZ = 4, 8, 8
N_SEQ = NX * NY
ROWS = D // N_SEQ
HALF = 3 * HD // 2
OWN = HD // 2
PIECE = HD // NY
EPS = 1e-05
F32, BF16 = jnp.float32, jnp.bfloat16
MESH = pl.DeviceIdType.MESH


def dot(a, b, ca, cb):
    return lax.dot_general(a, b, (((ca,), (cb,)), ((), ())), preferred_element_type=F32)


def far_first(n):
    return sorted(range(1, n), key=lambda k: (-min(k, n - k), k))


def kernel(
    x_ref, cot_ref, w_ref, out_ref, dx_ref, dw_ref,
    wbuf, acc, xsib, xt, gown, gsend, grads,
    sb, rb, tb, pb, state, sc, rc, tc, pc, suffix,
    part, q1, q1s, q2, q2s, k1, k1s, k2, k2s, v1, v1s, v2, v2s, last, fin,
    local_sem, a_send, ay, ax, ao, asib, xs_sem, b_send, br, c_send, cr,
    g_sem, d_send, dr, f_sem,
):
    dp, seq = lax.axis_index("dp"), lax.axis_index("seq")
    z, core = dp // 2, dp % 2
    x, y = seq // NY, seq % NY
    sib = (z * 2 + 1 - core, seq)
    pos = {"x": x, "y": y, "z": z}
    size = {"x": NX, "y": NY, "z": NZ}

    def at(axis, index):
        if axis == "x":
            return (dp, index * NY + y)
        if axis == "y":
            return (dp, x * NY + index)
        return (index * 2 + core, seq)

    def near(axis, k):
        return at(axis, (pos[axis] + k + size[axis]) % size[axis])

    def send(src, dst, s_sem, r_sem, device):
        pltpu.make_async_remote_copy(
            src_ref=src, dst_ref=dst, send_sem=s_sem, recv_sem=r_sem,
            device_id=device, device_id_type=MESH,
        ).start()

    def wait(ref, sem):
        pltpu.make_async_copy(ref, ref, sem).wait()

    def spread(axis, piece_for, landing, s_sem, r_sem):
        n, me = size[axis], pos[axis]
        for k in far_first(n):
            peer = (me + k) % n
            send(piece_for(peer), landing.at[me], s_sem, r_sem.at[k], at(axis, peer))

    def collect(axis, landing, r_sem):
        n, me = size[axis], pos[axis]
        for k in sorted(range(1, n), key=lambda k: min(k, n - k)):
            wait(landing.at[(me + n - k) % n], r_sem.at[k])

    barrier = pltpu.get_barrier_semaphore()
    peers = [sib]
    for axis in ("x", "y", "z"):
        peers += [near(axis, k) for k in range(1, size[axis])]
    for device in peers:
        pl.semaphore_signal(barrier, inc=1, device_id=device, device_id_type=MESH)
    pl.semaphore_wait(barrier, len(peers))

    mine = w_ref.at[:, pl.ds(pl.multiple_of(core * HALF, HALF), HALF)]
    low, high = pl.ds(0, ROWS // 2), pl.ds(ROWS // 2, ROWS // 2)

    def slot(dx, dy):
        return ((x + dx + NX) % NX) * NY + (y + dy + NY) % NY

    def pass_on(src, index, rows, axis, k, sem):
        send(src, wbuf.at[core, index, rows], a_send, sem, near(axis, k))

    whole = pl.ds(0, ROWS)

    def to_sibling(index, rows, block):
        ref = wbuf.at[core, index, rows]
        send(ref, ref, a_send, asib.at[block], sib)

    pass_on(mine, seq, whole, "x", 1, ax.at[0, 0])
    pass_on(mine, seq, whole, "x", -1, ax.at[1, 0])
    pass_on(mine, seq, whole, "y", 1, ay.at[0, 1])
    pass_on(mine, seq, whole, "y", -1, ay.at[1, 1])
    own_copies = []
    for half in range(2):
        copy = pltpu.make_async_copy(
            w_ref.at[:, pl.ds(half * HALF, HALF)], wbuf.at[half, seq], local_sem.at[half]
        )
        copy.start()
        own_copies.append(copy)
    send(x_ref, xsib, xs_sem.at[0], xs_sem.at[1], sib)

    def from_y(r):
        for way, step in ((0, 1), (1, -1)):
            index = slot(0, -step * r)
            rows = whole if r < NY // 2 else (low, high)[way]
            ref = wbuf.at[core, index, rows]
            wait(ref, ay.at[way, r])
            if r < NY // 2 - 1:
                pass_on(ref, index, whole, "y", step, ay.at[way, r + 1])
            elif r == NY // 2 - 1:
                part_rows = (low, high)[way]
                pass_on(wbuf.at[core, index, part_rows], index, part_rows, "y", step, ay.at[way, r + 1])
            if r < NY // 2 or way == 1:
                full = wbuf.at[core, index]
                k = (-step * r) % NY
                pass_on(full, index, whole, "x", 1, ax.at[0, k])
                pass_on(full, index, whole, "x", -1, ax.at[1, k])
                to_sibling(index, whole, 0)

    def offsets(r):
        return [0] if r == 0 else [NY // 2] if r == NY // 2 else [r, -r]

    def from_x(r):
        for k in offsets(r):
            for way, step in ((0, 1), (1, -1)):
                index = slot(-step, k)
                ref = wbuf.at[core, index]
                wait(ref, ax.at[way, k % NY])
                rows = (low, high)[way]
                pass_on(wbuf.at[core, index, rows], index, rows, "x", step, ao.at[way, k % NY])
                to_sibling(index, whole, 1 + way)

    def from_far(r):
        for k in offsets(r):
            index = slot(2, k)
            for way in range(2):
                wait(wbuf.at[core, index, (low, high)[way]], ao.at[way, k % NY])
            to_sibling(index, whole, 3)

    for r in range(1, 7):
        if r <= 4:
            from_y(r)
        if 1 <= r <= 5:
            from_x(r - 1)
        if 2 <= r:
            from_far(r - 2)

    for copy in own_copies:
        copy.wait()
    for block, dx in enumerate((0, -1, 1, 2)):
        xb = (x + dx + NX) % NX
        count = NY - 1 if block == 0 else NY
        wait(wbuf.at[0, pl.ds(0, count)], asib.at[block])
        features = x_ref[:, pl.ds(pl.multiple_of(xb * 256, 256), 256)]
        for half in range(2):
            weights = wbuf[half, pl.ds(xb * NY, NY)].reshape(256, HALF)
            term = dot(features, weights, 1, 0)
            if block == 0:
                acc[:, half * HALF : (half + 1) * HALF] = term
            else:
                acc[:, half * HALF : (half + 1) * HALF] += term
    proj = acc[...].astype(BF16)

    def head(part_index, h):
        start = part_index * HD + h * DH
        return proj[:, start : start + DH]

    query = [head(0, h) for h in range(HEADS)]
    key = [head(1, h) for h in range(HEADS)]
    value = [head(2, h) for h in range(HEADS)]
    rows_i = lax.broadcasted_iota(jnp.int32, (TOK, TOK), 0)
    cols_i = lax.broadcasted_iota(jnp.int32, (TOK, TOK), 1)
    causal = rows_i >= cols_i

    def scan_start(local, s_buf, r_buf, s_sem, r_sem):
        for h in range(HEADS):
            s_buf[2 * h : 2 * h + 2] = local[h].astype(BF16).reshape(2, PIECE, DH)
        spread("y", lambda p: s_buf.at[p], r_buf, s_sem.at[0], r_sem.at[0])
        r_buf[y] = s_buf[y]

    def scan_middle(r_buf, t_buf, s_sem, r_sem):
        collect("y", r_buf, r_sem.at[0])
        total = r_buf[0].astype(F32)
        for c in range(1, NY):
            total = total + r_buf[c].astype(F32)
        t_buf[x] = total.astype(BF16)
        spread("x", lambda p: t_buf.at[x], t_buf, s_sem.at[1], r_sem.at[1])

    def scan_end(r_buf, t_buf, p_buf, landing, s_sem, r_sem, reverse):
        collect("x", t_buf, r_sem.at[1])
        run = jnp.zeros((PIECE, DH), F32)
        for c in range(NX):
            ahead = c > x if reverse else c < x
            run = run + jnp.where(ahead, t_buf[c].astype(F32), 0.0)
        for c in reversed(range(NY)) if reverse else range(NY):
            p_buf[c] = run.astype(BF16)
            run = run + r_buf[c].astype(F32)
        spread("y", lambda p: p_buf.at[p], landing, s_sem.at[2], r_sem.at[2])
        landing[y] = p_buf[y]

    def scan_done(r_buf, t_buf, landing, s_sem, r_sem):
        collect("y", landing, r_sem.at[2])
        return [landing[2 * h : 2 * h + 2].reshape(DH, DH) for h in range(HEADS)]

    scan_start([dot(key[h], value[h], 0, 0) for h in range(HEADS)], sb, rb, b_send, br)
    scores = []
    mixed = []
    for h in range(HEADS):
        s = jnp.where(causal, dot(query[h], key[h], 1, 1), 0.0).astype(BF16)
        scores.append(s)
        mixed.append(dot(s, value[h], 1, 0))
    scan_middle(rb, tb, b_send, br)
    wait(xsib, xs_sem.at[1])
    xt[:, 0:TOK] = x_ref[...].T
    xt[:, TOK:] = xsib[...].T
    scan_end(rb, tb, pb, state, b_send, br, False)
    states = scan_done(rb, tb, state, b_send, br)

    grad = []
    for h in range(HEADS):
        m = mixed[h] + dot(query[h], states[h], 1, 0)
        scale = lax.rsqrt(jnp.mean(m * m, axis=-1, keepdims=True) + EPS)
        o = m * scale
        out_ref[:, h * DH : (h + 1) * DH] = o.astype(BF16)
        up = cot_ref[:, h * DH : (h + 1) * DH].astype(F32)
        grad.append((scale * (up - o * jnp.mean(up * o, axis=-1, keepdims=True))).astype(BF16))

    scan_start([dot(query[h], grad[h], 0, 0) for h in range(HEADS)], sc, rc, c_send, cr)

    def keep(group, h, value_f32):
        g = value_f32.astype(BF16)
        grads[:, group * HD + h * DH : group * HD + (h + 1) * DH] = g
        gsend[group, h // 2, :, (h % 2) * DH : (h % 2 + 1) * DH] = g

    def to_pair(group):
        gown[group, 0:TOK] = gsend[group, core]
        send(
            gsend.at[group, 1 - core], gown.at[group, pl.ds(TOK, TOK)],
            g_sem.at[0, group], g_sem.at[1, group], sib,
        )

    key_part, value_part = [], []
    for h in range(HEADS):
        back = jnp.where(causal, dot(grad[h], value[h], 1, 1), 0.0).astype(BF16)
        keep(0, h, dot(back, key[h], 1, 0) + dot(grad[h], states[h], 1, 1))
        key_part.append(dot(back, query[h], 0, 0))
        value_part.append(dot(scores[h], grad[h], 0, 0))
    to_pair(0)
    scan_middle(rc, tc, c_send, cr)

    def partial(group):
        wait(gown.at[group, pl.ds(TOK, TOK)], g_sem.at[1, group])
        p = dot(xt[...], gown[group], 1, 0).astype(BF16)
        part[group] = p.reshape(NX, NY, ROWS, OWN)

    def add_up(landing):
        total = landing[0].astype(F32)
        for c in range(1, landing.shape[0]):
            total = total + landing[c].astype(F32)
        return total

    def first_x(group, landing):
        spread("x", lambda p: part.at[group, p], landing, d_send.at[group, 0], dr.at[group, 0])
        landing[x] = part[group, x]

    def first_y(group, landing):
        spread("y", lambda p: part.at[group, :, p], landing, d_send.at[group, 0], dr.at[group, 0])
        landing[y] = part[group, :, y]

    def second(group, axis_in, landing_in, mid, axis, landing):
        collect(axis_in, landing_in, dr.at[group, 0])
        mid[...] = add_up(landing_in).astype(BF16)
        spread(axis, lambda p: mid.at[p], landing, d_send.at[group, 1], dr.at[group, 1])
        landing[pos[axis]] = mid[pos[axis]]

    def third(group, axis_in, landing_in, mid):
        collect(axis_in, landing_in, dr.at[group, 1])
        mid[...] = add_up(landing_in).astype(BF16)
        spread("z", lambda p: mid, last.at[group], d_send.at[group, 2], dr.at[group, 2])
        last[group, z] = mid[...]

    def finish(group):
        collect("z", last.at[group], dr.at[group, 2])
        fin[core, group] = add_up(last.at[group])
        send(fin.at[core, group], fin.at[core, group], f_sem.at[0, group], f_sem.at[1, group], sib)

    scan_end(rc, tc, pc, suffix, c_send, cr, True)
    partial(0)
    first_x(0, q1)
    suffixes = scan_done(rc, tc, suffix, c_send, cr)

    for h in range(HEADS):
        keep(1, h, key_part[h] + dot(value[h], suffixes[h], 1, 1))
    to_pair(1)
    for h in range(HEADS):
        keep(2, h, value_part[h] + dot(key[h], suffixes[h], 1, 0))
    to_pair(2)
    second(0, "x", q1, q1s, "y", q2)
    partial(2)
    first_y(2, v1)
    partial(1)
    first_x(1, k1)
    third(0, "y", q2, q2s)

    g = grads[...]
    dx = dot(g[:, :HALF], wbuf[0].reshape(D, HALF), 1, 1)
    dx = dx + dot(g[:, HALF:], wbuf[1].reshape(D, HALF), 1, 1)
    dx_ref[...] = dx.astype(BF16)

    second(1, "x", k1, k1s, "y", k2)
    finish(0)
    second(2, "y", v1, v1s, "x", v2)
    third(1, "y", k2, k2s)
    third(2, "x", v2, v2s)
    finish(1)
    finish(2)
    for group in range(3):
        wait(fin.at[1 - core, group], f_sem.at[1, group])
        for half in range(2):
            start = group * HD + half * OWN
            dw_ref[:, start : start + OWN] = fin[half, group]

    wait(wbuf.at[:, pl.ds(0, N_SEQ - 1)], a_send)
    wait(xsib, xs_sem.at[0])
    for s_sem in (b_send, c_send):
        wait(rb.at[pl.ds(0, NY - 1)], s_sem.at[0])
        wait(tb.at[pl.ds(0, NX - 1)], s_sem.at[1])
        wait(state.at[pl.ds(0, NY - 1)], s_sem.at[2])
    wait(q1.at[pl.ds(0, NX - 1)], d_send.at[0, 0])
    wait(q2.at[pl.ds(0, NY - 1)], d_send.at[0, 1])
    wait(k1.at[pl.ds(0, NX - 1)], d_send.at[1, 0])
    wait(k2.at[pl.ds(0, NY - 1)], d_send.at[1, 1])
    wait(v1.at[pl.ds(0, NY - 1)], d_send.at[2, 0])
    wait(v2.at[pl.ds(0, NX - 1)], d_send.at[2, 1])
    for group in range(3):
        wait(last.at[group, pl.ds(0, NZ - 1)], d_send.at[group, 2])
        wait(gsend.at[group, 0], g_sem.at[0, group])
        wait(fin.at[0, group], f_sem.at[0, group])


def shards(inputs, cotangent, qkv_weight):
    vmem = pl.BlockSpec(memory_space=pltpu.VMEM)
    dma = pltpu.SemaphoreType.DMA
    scan_bufs = [
        pltpu.VMEM((NY, PIECE, DH), BF16),
        pltpu.VMEM((NY, PIECE, DH), BF16),
        pltpu.VMEM((NX, PIECE, DH), BF16),
        pltpu.VMEM((NY, PIECE, DH), BF16),
        pltpu.VMEM((NY, PIECE, DH), BF16),
    ]
    x_bufs = [
        pltpu.VMEM((NX, NY, ROWS, OWN), BF16),
        pltpu.VMEM((NY, ROWS, OWN), BF16),
        pltpu.VMEM((NY, ROWS, OWN), BF16),
        pltpu.VMEM((ROWS, OWN), BF16),
    ]
    y_bufs = [
        pltpu.VMEM((NY, NX, ROWS, OWN), BF16),
        pltpu.VMEM((NX, ROWS, OWN), BF16),
        pltpu.VMEM((NX, ROWS, OWN), BF16),
        pltpu.VMEM((ROWS, OWN), BF16),
    ]
    out, dx, dw = pl.pallas_call(
        kernel,
        name="layer",
        out_shape=(
            jax.ShapeDtypeStruct((TOK, HD), BF16),
            jax.ShapeDtypeStruct((TOK, D), BF16),
            jax.ShapeDtypeStruct((ROWS, 3 * HD), F32),
        ),
        in_specs=[vmem] * 3,
        out_specs=(vmem,) * 3,
        scratch_shapes=[
            pltpu.VMEM((2, N_SEQ, ROWS, HALF), BF16),
            pltpu.VMEM((TOK, 3 * HD), F32),
            pltpu.VMEM((TOK, D), BF16),
            pltpu.VMEM((D, 2 * TOK), BF16),
            pltpu.VMEM((3, 2 * TOK, OWN), BF16),
            pltpu.VMEM((3, 2, TOK, OWN), BF16),
            pltpu.VMEM((TOK, 3 * HD), BF16),
            *scan_bufs,
            *scan_bufs,
            pltpu.VMEM((3, NX, NY, ROWS, OWN), BF16),
            *x_bufs,
            *x_bufs,
            *y_bufs,
            pltpu.VMEM((3, NZ, ROWS, OWN), BF16),
            pltpu.VMEM((2, 3, ROWS, OWN), F32),
            dma((2,)),
            dma(()),
            dma((2, 5)),
            dma((2, NY)),
            dma((2, NY)),
            dma((4,)),
            dma((2,)),
            dma((3,)),
            dma((3, NY)),
            dma((3,)),
            dma((3, NY)),
            dma((2, 3)),
            dma((3, 3)),
            dma((3, 3, NY)),
            dma((2, 3)),
        ],
        compiler_params=pltpu.CompilerParams(
            collective_id=0, has_side_effects=True, vmem_limit_bytes=48 * 1024 * 1024
        ),
    )(inputs[0], cotangent[0], qkv_weight)
    return out[None], dx[None], dw


def solution(mesh):
    in_specs = (P("dp", "seq", None), P("dp", "seq", None), P("seq", None))
    out_specs = (P("dp", "seq", None), P("dp", "seq", None), P("seq", None))
    return jax.shard_map(shards, mesh=mesh, in_specs=in_specs, out_specs=out_specs, check_vma=False)
```

```python
import jax
import jax.numpy as jnp
from jax import lax
from jax.experimental import pallas as pl
from jax.experimental.pallas import tpu as pltpu
from jax.sharding import PartitionSpec as P

HEADS, DH, TOK = 4, 128, 128
D, HD = 1024, 512
NX, NY, NZ = 4, 8, 8
N_SEQ = NX * NY
ROWS = D // N_SEQ
QUAD = 4
PIECE = QUAD * DH // NY
EPS = 1e-05
F32, BF16 = jnp.float32, jnp.bfloat16
MESH = pl.DeviceIdType.MESH


def dot(a, b, ca, cb):
    return lax.dot_general(a, b, (((ca,), (cb,)), ((), ())), preferred_element_type=F32)


def far_first(n):
    return sorted(range(1, n), key=lambda k: (-min(k, n - k), k))


def near_first(n):
    return sorted(range(1, n), key=lambda k: (min(k, n - k), k))


def kernel(
    x_ref, cot_ref, w_ref, out_ref, dx_ref, dw_ref,
    wbuf, acc, xall, xt, cots, outs, gq, gkv,
    sb, rb, tb, pb, state, sc, rc, tc, pc, suffix,
    part, q1, q1s, q2, q2s, k1, k1s, k2, k2s, v1, v1s, v2, v2s, last, fin,
    dxs, dxr, dxz, dxzr,
    load, a_send, ay, ax, x_send, x_recv, cot_send, cot_recv, out_send, out_recv,
    b_send, br, c_send, cr, d_send, dr, f_sem, dx_send, dx_recv,
):
    dp, seq = lax.axis_index("dp"), lax.axis_index("seq")
    z, core = dp // 2, dp % 2
    x, y = seq // NY, seq % NY
    zq = z % 2
    head = zq * 2 + core
    zmate = z + 1 - 2 * zq
    mate_dev = (zmate * 2 + core, seq)
    sib_dev = (z * 2 + 1 - core, seq)
    diag_dev = (zmate * 2 + 1 - core, seq)
    mate, sib, diag = (1 - zq) * 2 + core, zq * 2 + 1 - core, (1 - zq) * 2 + 1 - core
    pos = {"x": x, "y": y, "z": z}
    size = {"x": NX, "y": NY, "z": NZ}

    def at(axis, index):
        if axis == "x":
            return (dp, index * NY + y)
        if axis == "y":
            return (dp, x * NY + index)
        return (index * 2 + core, seq)

    def send(src, dst, s_sem, r_sem, device):
        pltpu.make_async_remote_copy(
            src_ref=src, dst_ref=dst, send_sem=s_sem, recv_sem=r_sem,
            device_id=device, device_id_type=MESH,
        ).start()

    def wait(ref, sem):
        pltpu.make_async_copy(ref, ref, sem).wait()

    def spread(axis, piece_for, landing, s_sem, r_sem):
        n, me = size[axis], pos[axis]
        for k in far_first(n):
            peer = (me + k) % n
            send(piece_for(peer), landing.at[me], s_sem, r_sem.at[k], at(axis, peer))

    def collect(axis, landing, r_sem):
        n, me = size[axis], pos[axis]
        for k in near_first(n):
            wait(landing.at[(me + n - k) % n], r_sem.at[k])

    loads = []
    for i in range(3):
        columns = pl.ds(pl.multiple_of(i * HD + head * DH, DH), DH)
        loads.append(
            pltpu.make_async_copy(
                w_ref.at[:, columns], wbuf.at[seq, :, pl.ds(i * DH, DH)], load.at[i]
            )
        )
    loads.append(pltpu.make_async_copy(x_ref, xall.at[head], load.at[3]))
    loads.append(
        pltpu.make_async_copy(
            cot_ref.at[:, pl.ds(pl.multiple_of(head * DH, DH), DH)], cots.at[head], load.at[4]
        )
    )
    for copy in loads:
        copy.start()

    barrier = pltpu.get_barrier_semaphore()
    peers = [sib_dev, diag_dev]
    for axis in ("x", "y", "z"):
        peers += [at(axis, (pos[axis] + k) % size[axis]) for k in range(1, size[axis])]
    for device in peers:
        pl.semaphore_signal(barrier, inc=1, device_id=device, device_id_type=MESH)
    for copy in loads[:3]:
        copy.wait()
    pl.semaphore_wait(barrier, len(peers))

    def weights_to(index, axis, k, sem):
        ref = wbuf.at[index]
        send(ref, ref, a_send, sem, at(axis, (pos[axis] + k) % size[axis]))

    for k in far_first(NY):
        weights_to(seq, "y", k, ay.at[k])
    for k in near_first(NX):
        weights_to(seq, "x", k, ax.at[k])
    send(x_ref, xall.at[head], x_send.at[0], x_recv.at[0], mate_dev)
    send(x_ref, xall.at[head], x_send.at[1], x_recv.at[1], sib_dev)
    for i, (place, device) in enumerate(((mate, mate_dev), (diag, diag_dev), (sib, sib_dev))):
        columns = pl.ds(pl.multiple_of(place * DH, DH), DH)
        send(cot_ref.at[:, columns], cots.at[head], cot_send.at[i], cot_recv.at[i], device)
    for k in near_first(NY):
        index = x * NY + (y + NY - k) % NY
        wait(wbuf.at[index], ay.at[k])
        for kx in near_first(NX):
            weights_to(index, "x", kx, ax.at[kx])
    wait(xall.at[mate], x_recv.at[0])
    send(xall.at[mate], xall.at[mate], x_send.at[2], x_recv.at[2], sib_dev)
    loads[3].wait()
    wait(xall.at[sib], x_recv.at[1])
    wait(xall.at[diag], x_recv.at[2])

    for kx in (0, 1, 3, 2):
        xb = (x + NX - kx) % NX
        block = wbuf.at[pl.ds(xb * NY, NY)]
        if kx:
            wait(block, ax.at[kx])
        features = xall[:, :, pl.ds(pl.multiple_of(xb * 256, 256), 256)].reshape(QUAD * TOK, 256)
        term = dot(features, block[...].reshape(256, 3 * DH), 1, 0)
        if kx == 0:
            acc[...] = term
        else:
            acc[...] += term
    proj = acc[...].astype(BF16)
    query, key, value = (
        [proj[j * TOK : (j + 1) * TOK, i * DH : (i + 1) * DH] for j in range(QUAD)] for i in range(3)
    )
    rows_i = lax.broadcasted_iota(jnp.int32, (TOK, TOK), 0)
    cols_i = lax.broadcasted_iota(jnp.int32, (TOK, TOK), 1)
    causal = rows_i >= cols_i

    def scan_start(local, s_buf, r_buf, s_sem, r_sem):
        for j in range(QUAD):
            s_buf[2 * j : 2 * j + 2] = local[j].astype(BF16).reshape(2, PIECE, DH)
        spread("y", lambda p: s_buf.at[p], r_buf, s_sem.at[0], r_sem.at[0])
        r_buf[y] = s_buf[y]

    def scan_middle(r_buf, t_buf, s_sem, r_sem):
        collect("y", r_buf, r_sem.at[0])
        total = r_buf[0].astype(F32)
        for c in range(1, NY):
            total = total + r_buf[c].astype(F32)
        t_buf[x] = total.astype(BF16)
        spread("x", lambda p: t_buf.at[x], t_buf, s_sem.at[1], r_sem.at[1])

    def scan_end(r_buf, t_buf, p_buf, landing, s_sem, r_sem, reverse):
        collect("x", t_buf, r_sem.at[1])
        run = jnp.zeros((PIECE, DH), F32)
        for c in range(NX):
            ahead = c > x if reverse else c < x
            run = run + jnp.where(ahead, t_buf[c].astype(F32), 0.0)
        for c in reversed(range(NY)) if reverse else range(NY):
            p_buf[c] = run.astype(BF16)
            run = run + r_buf[c].astype(F32)
        spread("y", lambda p: p_buf.at[p], landing, s_sem.at[2], r_sem.at[2])
        landing[y] = p_buf[y]

    def scan_done(landing, r_sem):
        collect("y", landing, r_sem.at[2])
        return [landing[2 * j : 2 * j + 2].reshape(DH, DH) for j in range(QUAD)]

    scan_start([dot(key[j], value[j], 0, 0) for j in range(QUAD)], sb, rb, b_send, br)
    scores = []
    mixed = []
    for j in range(QUAD):
        s = jnp.where(causal, dot(query[j], key[j], 1, 1), 0.0).astype(BF16)
        scores.append(s)
        mixed.append(dot(s, value[j], 1, 0))
    scan_middle(rb, tb, b_send, br)
    for j in range(QUAD):
        xt[:, j * TOK : (j + 1) * TOK] = xall[j].T
    scan_end(rb, tb, pb, state, b_send, br, False)
    loads[4].wait()
    for i, place in enumerate((mate, diag, sib)):
        wait(cots.at[place], cot_recv.at[i])
    states = scan_done(state, br)

    grad = []
    for j in range(QUAD):
        m = mixed[j] + dot(query[j], states[j], 1, 0)
        scale = lax.rsqrt(jnp.mean(m * m, axis=-1, keepdims=True) + EPS)
        o = m * scale
        outs[0, j] = o.astype(BF16)
        up = cots[j].astype(F32)
        grad.append((scale * (up - o * jnp.mean(up * o, axis=-1, keepdims=True))).astype(BF16))

    scan_start([dot(query[j], grad[j], 0, 0) for j in range(QUAD)], sc, rc, c_send, cr)
    for i, (place, device) in enumerate(((mate, mate_dev), (diag, diag_dev), (sib, sib_dev))):
        send(outs.at[0, place], outs.at[1, head], out_send.at[i], out_recv.at[i], device)
    outs[1, head] = outs[0, head]

    key_part, value_part = [], []
    for j in range(QUAD):
        back = jnp.where(causal, dot(grad[j], value[j], 1, 1), 0.0).astype(BF16)
        gq[j * TOK : (j + 1) * TOK, :] = (
            dot(back, key[j], 1, 0) + dot(grad[j], states[j], 1, 1)
        ).astype(BF16)
        key_part.append(dot(back, query[j], 0, 0))
        value_part.append(dot(scores[j], grad[j], 0, 0))
    scan_middle(rc, tc, c_send, cr)

    def add_up(landing, start=0, step=1):
        total = landing[start].astype(F32)
        for c in range(start + step, landing.shape[0], step):
            total = total + landing[c].astype(F32)
        return total

    def first_x(group, landing):
        spread("x", lambda p: part.at[group, p], landing, d_send.at[group, 0], dr.at[group, 0])
        landing[x] = part[group, x]

    def first_y(group, landing):
        spread("y", lambda p: part.at[group, :, p], landing, d_send.at[group, 0], dr.at[group, 0])
        landing[y] = part[group, :, y]

    def second(group, axis_in, landing_in, mid, axis, landing):
        collect(axis_in, landing_in, dr.at[group, 0])
        mid[...] = add_up(landing_in).astype(BF16)
        spread(axis, lambda p: mid.at[p], landing, d_send.at[group, 1], dr.at[group, 1])
        landing[pos[axis]] = mid[pos[axis]]

    def third(group, axis_in, landing_in, mid):
        collect(axis_in, landing_in, dr.at[group, 1])
        mid[...] = add_up(landing_in).astype(BF16)
        spread("z", lambda p: mid, last.at[group], d_send.at[group, 2], dr.at[group, 2])
        last[group, z] = mid[...]

    def finish(group):
        collect("z", last.at[group], dr.at[group, 2])
        for way in range(2):
            fin[core, group, way] = add_up(last.at[group], way, 2)
        ref = fin.at[core, group]
        send(ref, ref, f_sem.at[0, group], f_sem.at[1, group], sib_dev)

    part[0] = dot(xt[...], gq[...], 1, 0).astype(BF16).reshape(NX, NY, ROWS, DH)
    scan_end(rc, tc, pc, suffix, c_send, cr, True)
    first_x(0, q1)
    suffixes = scan_done(suffix, cr)

    for j in range(QUAD):
        gkv[j * TOK : (j + 1) * TOK, 0:DH] = (
            key_part[j] + dot(value[j], suffixes[j], 1, 1)
        ).astype(BF16)
        gkv[j * TOK : (j + 1) * TOK, DH:] = (
            value_part[j] + dot(key[j], suffixes[j], 1, 0)
        ).astype(BF16)
    both = dot(xt[...], gkv[...], 1, 0).astype(BF16)
    part[2] = both[:, DH:].reshape(NX, NY, ROWS, DH)
    first_y(2, v1)
    part[1] = both[:, :DH].reshape(NX, NY, ROWS, DH)
    first_x(1, k1)
    second(0, "x", q1, q1s, "y", q2)

    weights = wbuf[...].reshape(D, 3 * DH)

    def dx_term(j):
        start = pl.ds(pl.multiple_of(j * TOK, TOK), TOK)
        g = jnp.concatenate([gq[start, :], gkv[start, :]], axis=1)
        return dot(g, weights, 1, 1)

    dxs[0] = dx_term(diag).astype(BF16)
    send(dxs.at[0], dxr.at[0], dx_send.at[0], dx_recv.at[0], sib_dev)
    dxs[1] = dx_term(sib).astype(BF16)
    send(dxs.at[1], dxr.at[1], dx_send.at[1], dx_recv.at[1], sib_dev)
    to_mate = dx_term(mate)
    wait(dxr.at[0], dx_recv.at[0])
    dxz[...] = (to_mate + dxr[0].astype(F32)).astype(BF16)
    send(dxz, dxzr, dx_send.at[2], dx_recv.at[2], mate_dev)

    second(1, "x", k1, k1s, "y", k2)
    second(2, "y", v1, v1s, "x", v2)
    third(0, "y", q2, q2s)
    third(1, "y", k2, k2s)
    third(2, "x", v2, v2s)

    own = dx_term(head)
    wait(dxr.at[1], dx_recv.at[1])
    wait(dxzr, dx_recv.at[2])
    dx_ref[...] = (own + dxr[1].astype(F32) + dxzr[...].astype(F32)).astype(BF16)
    for i, place in enumerate((mate, diag, sib)):
        wait(outs.at[1, place], out_recv.at[i])
    for h in range(HEADS):
        out_ref[:, h * DH : (h + 1) * DH] = outs[1, h]

    finish(0)
    finish(1)
    finish(2)
    for group in range(3):
        wait(fin.at[1 - core, group], f_sem.at[1, group])
        for h in range(HEADS):
            start = group * HD + h * DH
            dw_ref[:, start : start + DH] = fin[h % 2, group, h // 2]

    wait(wbuf.at[pl.ds(0, N_SEQ - 1)], a_send)
    for i in range(3):
        wait(xall.at[0], x_send.at[i])
        wait(cots.at[0], cot_send.at[i])
        wait(outs.at[0, 0], out_send.at[i])
        wait(dxz, dx_send.at[i])
    for s_sem in (b_send, c_send):
        wait(rb.at[pl.ds(0, NY - 1)], s_sem.at[0])
        wait(tb.at[pl.ds(0, NX - 1)], s_sem.at[1])
        wait(state.at[pl.ds(0, NY - 1)], s_sem.at[2])
    wait(q1.at[pl.ds(0, NX - 1)], d_send.at[0, 0])
    wait(q2.at[pl.ds(0, NY - 1)], d_send.at[0, 1])
    wait(k1.at[pl.ds(0, NX - 1)], d_send.at[1, 0])
    wait(k2.at[pl.ds(0, NY - 1)], d_send.at[1, 1])
    wait(v1.at[pl.ds(0, NY - 1)], d_send.at[2, 0])
    wait(v2.at[pl.ds(0, NX - 1)], d_send.at[2, 1])
    for group in range(3):
        wait(last.at[group, pl.ds(0, NZ - 1)], d_send.at[group, 2])
        wait(fin.at[0, group], f_sem.at[0, group])


def shards(inputs, cotangent, qkv_weight):
    vmem = pl.BlockSpec(memory_space=pltpu.VMEM)
    hbm = pl.BlockSpec(memory_space=pltpu.HBM)
    dma = pltpu.SemaphoreType.DMA
    scan_bufs = [
        pltpu.VMEM((NY, PIECE, DH), BF16),
        pltpu.VMEM((NY, PIECE, DH), BF16),
        pltpu.VMEM((NX, PIECE, DH), BF16),
        pltpu.VMEM((NY, PIECE, DH), BF16),
        pltpu.VMEM((NY, PIECE, DH), BF16),
    ]
    x_bufs = [
        pltpu.VMEM((NX, NY, ROWS, DH), BF16),
        pltpu.VMEM((NY, ROWS, DH), BF16),
        pltpu.VMEM((NY, ROWS, DH), BF16),
        pltpu.VMEM((ROWS, DH), BF16),
    ]
    y_bufs = [
        pltpu.VMEM((NY, NX, ROWS, DH), BF16),
        pltpu.VMEM((NX, ROWS, DH), BF16),
        pltpu.VMEM((NX, ROWS, DH), BF16),
        pltpu.VMEM((ROWS, DH), BF16),
    ]
    out, dx, dw = pl.pallas_call(
        kernel,
        name="layer",
        out_shape=(
            jax.ShapeDtypeStruct((TOK, HD), BF16),
            jax.ShapeDtypeStruct((TOK, D), BF16),
            jax.ShapeDtypeStruct((ROWS, 3 * HD), F32),
        ),
        in_specs=[hbm] * 3,
        out_specs=(vmem,) * 3,
        scratch_shapes=[
            pltpu.VMEM((N_SEQ, ROWS, 3 * DH), BF16),
            pltpu.VMEM((QUAD * TOK, 3 * DH), F32),
            pltpu.VMEM((QUAD, TOK, D), BF16),
            pltpu.VMEM((D, QUAD * TOK), BF16),
            pltpu.VMEM((QUAD, TOK, DH), BF16),
            pltpu.VMEM((2, QUAD, TOK, DH), BF16),
            pltpu.VMEM((QUAD * TOK, DH), BF16),
            pltpu.VMEM((QUAD * TOK, 2 * DH), BF16),
            *scan_bufs,
            *scan_bufs,
            pltpu.VMEM((3, NX, NY, ROWS, DH), BF16),
            *x_bufs,
            *x_bufs,
            *y_bufs,
            pltpu.VMEM((3, NZ, ROWS, DH), BF16),
            pltpu.VMEM((2, 3, 2, ROWS, DH), F32),
            pltpu.VMEM((2, TOK, D), BF16),
            pltpu.VMEM((2, TOK, D), BF16),
            pltpu.VMEM((TOK, D), BF16),
            pltpu.VMEM((TOK, D), BF16),
            dma((5,)),
            dma(()),
            dma((NY,)),
            dma((NX,)),
            dma((3,)),
            dma((3,)),
            dma((3,)),
            dma((3,)),
            dma((3,)),
            dma((3,)),
            dma((3,)),
            dma((3, NY)),
            dma((3,)),
            dma((3, NY)),
            dma((3, 3)),
            dma((3, 3, NY)),
            dma((2, 3)),
            dma((3,)),
            dma((3,)),
        ],
        compiler_params=pltpu.CompilerParams(
            collective_id=0, has_side_effects=True, vmem_limit_bytes=40 * 1024 * 1024
        ),
    )(inputs[0], cotangent[0], qkv_weight)
    return out[None], dx[None], dw


def solution(mesh):
    in_specs = (P("dp", "seq", None), P("dp", "seq", None), P("seq", None))
    out_specs = (P("dp", "seq", None), P("dp", "seq", None), P("seq", None))
    return jax.shard_map(shards, mesh=mesh, in_specs=in_specs, out_specs=out_specs, check_vma=False)
```

```python
import jax
import jax.numpy as jnp
from jax import lax
from jax.experimental import pallas as pl
from jax.experimental.pallas import tpu as pltpu
from jax.sharding import PartitionSpec as P

HEADS, DH, TOK = 4, 128, 128
D, HD = 1024, 512
NX, NY, NZ = 4, 8, 8
N_SEQ = NX * NY
ROWS = D // N_SEQ
QUAD = 4
PIECE = QUAD * DH // NY
EPS = 1e-05
F32, BF16 = jnp.float32, jnp.bfloat16
MESH = pl.DeviceIdType.MESH


def dot(a, b, ca, cb):
    return lax.dot_general(a, b, (((ca,), (cb,)), ((), ())), preferred_element_type=F32)


def far_first(n):
    return sorted(range(1, n), key=lambda k: (-min(k, n - k), k))


def near_first(n):
    return sorted(range(1, n), key=lambda k: (min(k, n - k), k))


def kernel(
    x_ref, cot_ref, w_ref, out_ref, dx_ref, dw_ref,
    wq, wkv, accq, acckv, xall, xt, cots, outs, gq, gkv,
    sb, rb, tb, pb, state, sc, rc, tc, pc, suffix,
    part, q1, q1s, q2, q2s, k1, k1s, k2, k2s, v1, v1s, v2, v2s, last, fin,
    dxs, dxr, dxz, dxzr,
    load, aq_send, akv_send, aqy, aqx, akvy, akvx, x_send, x_recv, cot_send, cot_recv, out_send, out_recv,
    b_send, br, c_send, cr, d_send, dr, f_sem, dx_send, dx_recv,
):
    dp, seq = lax.axis_index("dp"), lax.axis_index("seq")
    z, core = dp // 2, dp % 2
    x, y = seq // NY, seq % NY
    zq = z % 2
    head = zq * 2 + core
    zmate = z + 1 - 2 * zq
    mate_dev = (zmate * 2 + core, seq)
    sib_dev = (z * 2 + 1 - core, seq)
    diag_dev = (zmate * 2 + 1 - core, seq)
    mate, sib, diag = (1 - zq) * 2 + core, zq * 2 + 1 - core, (1 - zq) * 2 + 1 - core
    pos = {"x": x, "y": y, "z": z}
    size = {"x": NX, "y": NY, "z": NZ}

    def at(axis, index):
        if axis == "x":
            return (dp, index * NY + y)
        if axis == "y":
            return (dp, x * NY + index)
        return (index * 2 + core, seq)

    def send(src, dst, s_sem, r_sem, device):
        pltpu.make_async_remote_copy(
            src_ref=src, dst_ref=dst, send_sem=s_sem, recv_sem=r_sem,
            device_id=device, device_id_type=MESH,
        ).start()

    def wait(ref, sem):
        pltpu.make_async_copy(ref, ref, sem).wait()

    def spread(axis, piece_for, landing, s_sem, r_sem):
        n, me = size[axis], pos[axis]
        for k in far_first(n):
            peer = (me + k) % n
            send(piece_for(peer), landing.at[me], s_sem, r_sem.at[k], at(axis, peer))

    def collect(axis, landing, r_sem):
        n, me = size[axis], pos[axis]
        for k in near_first(n):
            wait(landing.at[(me + n - k) % n], r_sem.at[k])

    loads = []
    for i in range(3):
        columns = pl.ds(pl.multiple_of(i * HD + head * DH, DH), DH)
        loads.append(
            pltpu.make_async_copy(
                w_ref.at[:, columns],
                wkv.at[seq, :, pl.ds((i - 1) * DH, DH)] if i else wq.at[seq],
                load.at[i],
            )
        )
    loads.append(pltpu.make_async_copy(x_ref, xall.at[head], load.at[3]))
    loads.append(
        pltpu.make_async_copy(
            cot_ref.at[:, pl.ds(pl.multiple_of(head * DH, DH), DH)], cots.at[head], load.at[4]
        )
    )
    for copy in loads:
        copy.start()

    barrier = pltpu.get_barrier_semaphore()
    peers = [sib_dev, diag_dev]
    for axis in ("x", "y", "z"):
        peers += [at(axis, (pos[axis] + k) % size[axis]) for k in range(1, size[axis])]
    for device in peers:
        pl.semaphore_signal(barrier, inc=1, device_id=device, device_id_type=MESH)
    for copy in loads[:3]:
        copy.wait()
    pl.semaphore_wait(barrier, len(peers))

    key_value = (wkv, akv_send, akvy, akvx)
    queries = (wq, aq_send, aqy, aqx)

    def weights_to(group, index, axis, k):
        ref = group[0].at[index]
        send(ref, ref, group[1], group[3 if axis == "x" else 2].at[k], at(axis, (pos[axis] + k) % size[axis]))

    def weights_start(group):
        for k in near_first(NY):
            weights_to(group, seq, "y", k)
        for k in near_first(NX):
            weights_to(group, seq, "x", k)

    def weights_forward(group):
        for k in near_first(NY):
            index = x * NY + (y + NY - k) % NY
            wait(group[0].at[index], group[2].at[k])
            for kx in near_first(NX):
                weights_to(group, index, "x", kx)

    weights_start(key_value)
    halves = [pl.ds(i * (TOK // 2), TOK // 2) for i in range(2)]
    for i in range(2):
        send(x_ref.at[halves[i]], xall.at[head, halves[i]], x_send.at[0], x_recv.at[0, i], mate_dev)
    send(x_ref, xall.at[head], x_send.at[1], x_recv.at[1, 0], sib_dev)
    weights_start(queries)
    for i, (place, device) in enumerate(((mate, mate_dev), (diag, diag_dev), (sib, sib_dev))):
        columns = pl.ds(pl.multiple_of(place * DH, DH), DH)
        send(cot_ref.at[:, columns], cots.at[head], cot_send.at[i], cot_recv.at[i], device)
    weights_forward(key_value)
    for i in range(2):
        ref = xall.at[mate, halves[i]]
        wait(ref, x_recv.at[0, i])
        send(ref, ref, x_send.at[2], x_recv.at[2, i], sib_dev)
    weights_forward(queries)
    loads[3].wait()
    wait(xall.at[sib], x_recv.at[1, 0])
    for i in range(2):
        wait(xall.at[diag, halves[i]], x_recv.at[2, i])

    def project(group, total):
        for kx in (0, 1, 3, 2):
            xb = (x + NX - kx) % NX
            block = group[0].at[pl.ds(xb * NY, NY)]
            if kx:
                wait(block, group[3].at[kx])
            features = xall[:, :, pl.ds(pl.multiple_of(xb * 256, 256), 256)].reshape(QUAD * TOK, 256)
            term = dot(features, block[...].reshape(256, -1), 1, 0)
            if kx == 0:
                total[...] = term
            else:
                total[...] += term
        proj = total[...].astype(BF16)
        return [
            [proj[j * TOK : (j + 1) * TOK, i : i + DH] for j in range(QUAD)]
            for i in range(0, proj.shape[1], DH)
        ]

    key, value = project(key_value, acckv)
    rows_i = lax.broadcasted_iota(jnp.int32, (TOK, TOK), 0)
    cols_i = lax.broadcasted_iota(jnp.int32, (TOK, TOK), 1)
    causal = rows_i >= cols_i

    def scan_start(local, s_buf, r_buf, s_sem, r_sem):
        for j in range(QUAD):
            s_buf[2 * j : 2 * j + 2] = local[j].astype(BF16).reshape(2, PIECE, DH)
        spread("y", lambda p: s_buf.at[p], r_buf, s_sem.at[0], r_sem.at[0])
        r_buf[y] = s_buf[y]

    def scan_middle(r_buf, t_buf, s_sem, r_sem):
        collect("y", r_buf, r_sem.at[0])
        total = r_buf[0].astype(F32)
        for c in range(1, NY):
            total = total + r_buf[c].astype(F32)
        t_buf[x] = total.astype(BF16)
        spread("x", lambda p: t_buf.at[x], t_buf, s_sem.at[1], r_sem.at[1])

    def scan_end(r_buf, t_buf, p_buf, landing, s_sem, r_sem, reverse):
        collect("x", t_buf, r_sem.at[1])
        run = jnp.zeros((PIECE, DH), F32)
        for c in range(NX):
            ahead = c > x if reverse else c < x
            run = run + jnp.where(ahead, t_buf[c].astype(F32), 0.0)
        for c in reversed(range(NY)) if reverse else range(NY):
            p_buf[c] = run.astype(BF16)
            run = run + r_buf[c].astype(F32)
        spread("y", lambda p: p_buf.at[p], landing, s_sem.at[2], r_sem.at[2])
        landing[y] = p_buf[y]

    def scan_done(landing, r_sem):
        collect("y", landing, r_sem.at[2])
        return [landing[2 * j : 2 * j + 2].reshape(DH, DH) for j in range(QUAD)]

    scan_start([dot(key[j], value[j], 0, 0) for j in range(QUAD)], sb, rb, b_send, br)
    (query,) = project(queries, accq)
    scores = []
    mixed = []
    for j in range(QUAD):
        s = jnp.where(causal, dot(query[j], key[j], 1, 1), 0.0).astype(BF16)
        scores.append(s)
        mixed.append(dot(s, value[j], 1, 0))
    scan_middle(rb, tb, b_send, br)
    for j in range(QUAD):
        xt[:, j * TOK : (j + 1) * TOK] = xall[j].T
    scan_end(rb, tb, pb, state, b_send, br, False)
    loads[4].wait()
    for i, place in enumerate((mate, diag, sib)):
        wait(cots.at[place], cot_recv.at[i])
    states = scan_done(state, br)

    grad = []
    for j in range(QUAD):
        m = mixed[j] + dot(query[j], states[j], 1, 0)
        scale = lax.rsqrt(jnp.mean(m * m, axis=-1, keepdims=True) + EPS)
        o = m * scale
        outs[0, j] = o.astype(BF16)
        up = cots[j].astype(F32)
        grad.append((scale * (up - o * jnp.mean(up * o, axis=-1, keepdims=True))).astype(BF16))

    scan_start([dot(query[j], grad[j], 0, 0) for j in range(QUAD)], sc, rc, c_send, cr)
    for i, (place, device) in enumerate(((mate, mate_dev), (diag, diag_dev), (sib, sib_dev))):
        send(outs.at[0, place], outs.at[1, head], out_send.at[i], out_recv.at[i], device)
    outs[1, head] = outs[0, head]

    key_part, value_part = [], []
    for j in range(QUAD):
        back = jnp.where(causal, dot(grad[j], value[j], 1, 1), 0.0).astype(BF16)
        gq[j * TOK : (j + 1) * TOK, :] = (
            dot(back, key[j], 1, 0) + dot(grad[j], states[j], 1, 1)
        ).astype(BF16)
        key_part.append(dot(back, query[j], 0, 0))
        value_part.append(dot(scores[j], grad[j], 0, 0))
    scan_middle(rc, tc, c_send, cr)

    def add_up(landing, start=0, step=1):
        total = landing[start].astype(F32)
        for c in range(start + step, landing.shape[0], step):
            total = total + landing[c].astype(F32)
        return total

    def first_x(group, landing):
        spread("x", lambda p: part.at[group, p], landing, d_send.at[group, 0], dr.at[group, 0])
        landing[x] = part[group, x]

    def first_y(group, landing):
        spread("y", lambda p: part.at[group, :, p], landing, d_send.at[group, 0], dr.at[group, 0])
        landing[y] = part[group, :, y]

    def second(group, axis_in, landing_in, mid, axis, landing):
        collect(axis_in, landing_in, dr.at[group, 0])
        mid[...] = add_up(landing_in).astype(BF16)
        spread(axis, lambda p: mid.at[p], landing, d_send.at[group, 1], dr.at[group, 1])
        landing[pos[axis]] = mid[pos[axis]]

    def third(group, axis_in, landing_in, mid):
        collect(axis_in, landing_in, dr.at[group, 1])
        mid[...] = add_up(landing_in).astype(BF16)
        spread("z", lambda p: mid, last.at[group], d_send.at[group, 2], dr.at[group, 2])
        last[group, z] = mid[...]

    def finish(group):
        collect("z", last.at[group], dr.at[group, 2])
        for way in range(2):
            fin[core, group, way] = add_up(last.at[group], way, 2)
        ref = fin.at[core, group]
        send(ref, ref, f_sem.at[0, group], f_sem.at[1, group], sib_dev)

    part[0] = dot(xt[...], gq[...], 1, 0).astype(BF16).reshape(NX, NY, ROWS, DH)
    scan_end(rc, tc, pc, suffix, c_send, cr, True)
    first_x(0, q1)
    suffixes = scan_done(suffix, cr)

    for j in range(QUAD):
        gkv[j * TOK : (j + 1) * TOK, 0:DH] = (
            key_part[j] + dot(value[j], suffixes[j], 1, 1)
        ).astype(BF16)
        gkv[j * TOK : (j + 1) * TOK, DH:] = (
            value_part[j] + dot(key[j], suffixes[j], 1, 0)
        ).astype(BF16)
    both = dot(xt[...], gkv[...], 1, 0).astype(BF16)
    part[2] = both[:, DH:].reshape(NX, NY, ROWS, DH)
    first_y(2, v1)
    part[1] = both[:, :DH].reshape(NX, NY, ROWS, DH)
    first_x(1, k1)
    second(0, "x", q1, q1s, "y", q2)

    def dx_term(j):
        start = pl.ds(pl.multiple_of(j * TOK, TOK), TOK)
        return dot(gq[start, :], wq[...].reshape(D, DH), 1, 1) + dot(
            gkv[start, :], wkv[...].reshape(D, 2 * DH), 1, 1
        )

    dxs[0] = dx_term(diag).astype(BF16)
    send(dxs.at[0], dxr.at[0], dx_send.at[0], dx_recv.at[0], sib_dev)
    dxs[1] = dx_term(sib).astype(BF16)
    send(dxs.at[1], dxr.at[1], dx_send.at[1], dx_recv.at[1], sib_dev)
    to_mate = dx_term(mate)
    wait(dxr.at[0], dx_recv.at[0])
    dxz[...] = (to_mate + dxr[0].astype(F32)).astype(BF16)
    send(dxz, dxzr, dx_send.at[2], dx_recv.at[2], mate_dev)

    second(1, "x", k1, k1s, "y", k2)
    second(2, "y", v1, v1s, "x", v2)
    third(0, "y", q2, q2s)
    third(1, "y", k2, k2s)
    third(2, "x", v2, v2s)

    own = dx_term(head)
    wait(dxr.at[1], dx_recv.at[1])
    wait(dxzr, dx_recv.at[2])
    dx_ref[...] = (own + dxr[1].astype(F32) + dxzr[...].astype(F32)).astype(BF16)
    for i, place in enumerate((mate, diag, sib)):
        wait(outs.at[1, place], out_recv.at[i])
    for h in range(HEADS):
        out_ref[:, h * DH : (h + 1) * DH] = outs[1, h]

    finish(0)
    finish(1)
    finish(2)
    for group in range(3):
        wait(fin.at[1 - core, group], f_sem.at[1, group])
        for h in range(HEADS):
            start = group * HD + h * DH
            dw_ref[:, start : start + DH] = fin[h % 2, group, h // 2]

    wait(wq.at[pl.ds(0, N_SEQ - 1)], aq_send)
    wait(wkv.at[pl.ds(0, N_SEQ - 1)], akv_send)
    for i in range(3):
        wait(xall.at[0], x_send.at[i])
        wait(cots.at[0], cot_send.at[i])
        wait(outs.at[0, 0], out_send.at[i])
        wait(dxz, dx_send.at[i])
    for s_sem in (b_send, c_send):
        wait(rb.at[pl.ds(0, NY - 1)], s_sem.at[0])
        wait(tb.at[pl.ds(0, NX - 1)], s_sem.at[1])
        wait(state.at[pl.ds(0, NY - 1)], s_sem.at[2])
    wait(q1.at[pl.ds(0, NX - 1)], d_send.at[0, 0])
    wait(q2.at[pl.ds(0, NY - 1)], d_send.at[0, 1])
    wait(k1.at[pl.ds(0, NX - 1)], d_send.at[1, 0])
    wait(k2.at[pl.ds(0, NY - 1)], d_send.at[1, 1])
    wait(v1.at[pl.ds(0, NY - 1)], d_send.at[2, 0])
    wait(v2.at[pl.ds(0, NX - 1)], d_send.at[2, 1])
    for group in range(3):
        wait(last.at[group, pl.ds(0, NZ - 1)], d_send.at[group, 2])
        wait(fin.at[0, group], f_sem.at[0, group])


def store(a_ref, b_ref, c_ref, a_out, b_out, c_out, sems):
    copies = [
        pltpu.make_async_copy(src, dst, sems.at[i])
        for i, (src, dst) in enumerate(((a_ref, a_out), (b_ref, b_out), (c_ref, c_out)))
    ]
    for copy in copies:
        copy.start()
    for copy in copies:
        copy.wait()


def shards(inputs, cotangent, qkv_weight):
    vmem = pl.BlockSpec(memory_space=pltpu.VMEM)
    hbm = pl.BlockSpec(memory_space=pltpu.HBM)
    dma = pltpu.SemaphoreType.DMA
    scan_bufs = [
        pltpu.VMEM((NY, PIECE, DH), BF16),
        pltpu.VMEM((NY, PIECE, DH), BF16),
        pltpu.VMEM((NX, PIECE, DH), BF16),
        pltpu.VMEM((NY, PIECE, DH), BF16),
        pltpu.VMEM((NY, PIECE, DH), BF16),
    ]
    x_bufs = [
        pltpu.VMEM((NX, NY, ROWS, DH), BF16),
        pltpu.VMEM((NY, ROWS, DH), BF16),
        pltpu.VMEM((NY, ROWS, DH), BF16),
        pltpu.VMEM((ROWS, DH), BF16),
    ]
    y_bufs = [
        pltpu.VMEM((NY, NX, ROWS, DH), BF16),
        pltpu.VMEM((NX, ROWS, DH), BF16),
        pltpu.VMEM((NX, ROWS, DH), BF16),
        pltpu.VMEM((ROWS, DH), BF16),
    ]
    out, dx, dw = pl.pallas_call(
        kernel,
        name="layer",
        out_shape=(
            jax.ShapeDtypeStruct((TOK, HD), BF16),
            jax.ShapeDtypeStruct((TOK, D), BF16),
            jax.ShapeDtypeStruct((ROWS, 3 * HD), F32),
        ),
        in_specs=[hbm] * 3,
        out_specs=(vmem,) * 3,
        scratch_shapes=[
            pltpu.VMEM((N_SEQ, ROWS, DH), BF16),
            pltpu.VMEM((N_SEQ, ROWS, 2 * DH), BF16),
            pltpu.VMEM((QUAD * TOK, DH), F32),
            pltpu.VMEM((QUAD * TOK, 2 * DH), F32),
            pltpu.VMEM((QUAD, TOK, D), BF16),
            pltpu.VMEM((D, QUAD * TOK), BF16),
            pltpu.VMEM((QUAD, TOK, DH), BF16),
            pltpu.VMEM((2, QUAD, TOK, DH), BF16),
            pltpu.VMEM((QUAD * TOK, DH), BF16),
            pltpu.VMEM((QUAD * TOK, 2 * DH), BF16),
            *scan_bufs,
            *scan_bufs,
            pltpu.VMEM((3, NX, NY, ROWS, DH), BF16),
            *x_bufs,
            *x_bufs,
            *y_bufs,
            pltpu.VMEM((3, NZ, ROWS, DH), BF16),
            pltpu.VMEM((2, 3, 2, ROWS, DH), F32),
            pltpu.VMEM((2, TOK, D), BF16),
            pltpu.VMEM((2, TOK, D), BF16),
            pltpu.VMEM((TOK, D), BF16),
            pltpu.VMEM((TOK, D), BF16),
            dma((5,)),
            dma(()),
            dma(()),
            dma((NY,)),
            dma((NX,)),
            dma((NY,)),
            dma((NX,)),
            dma((3,)),
            dma((3, 2)),
            dma((3,)),
            dma((3,)),
            dma((3,)),
            dma((3,)),
            dma((3,)),
            dma((3, NY)),
            dma((3,)),
            dma((3, NY)),
            dma((3, 3)),
            dma((3, 3, NY)),
            dma((2, 3)),
            dma((3,)),
            dma((3,)),
        ],
        compiler_params=pltpu.CompilerParams(
            collective_id=0, has_side_effects=True, vmem_limit_bytes=40 * 1024 * 1024
        ),
    )(*(pltpu.with_memory_space_constraint(a, pltpu.HBM) for a in (inputs[0], cotangent[0], qkv_weight)))
    out, dx, dw = pl.pallas_call(
        store,
        name="store",
        out_shape=(
            jax.ShapeDtypeStruct((TOK, HD), BF16),
            jax.ShapeDtypeStruct((TOK, D), BF16),
            jax.ShapeDtypeStruct((ROWS, 3 * HD), F32),
        ),
        in_specs=[vmem] * 3,
        out_specs=(hbm,) * 3,
        scratch_shapes=[dma((3,))],
        compiler_params=pltpu.CompilerParams(vmem_limit_bytes=4 * 1024 * 1024),
    )(out, dx, dw)
    return out[None], dx[None], dw


def solution(mesh):
    in_specs = (P("dp", "seq", None), P("dp", "seq", None), P("seq", None))
    out_specs = (P("dp", "seq", None), P("dp", "seq", None), P("seq", None))
    return jax.shard_map(shards, mesh=mesh, in_specs=in_specs, out_specs=out_specs, check_vma=False)
```

```python
import jax
import jax.numpy as jnp
from jax import lax
from jax.experimental import pallas as pl
from jax.experimental.pallas import tpu as pltpu
from jax.sharding import PartitionSpec as P

HEADS, DH, TOK = 4, 128, 128
D, HD = 1024, 512
NX, NY, NZ = 4, 8, 8
N_SEQ = NX * NY
ROWS = D // N_SEQ
QUAD = 4
PIECE = QUAD * DH // N_SEQ
EPS = 1e-05
F32, BF16 = jnp.float32, jnp.bfloat16
MESH = pl.DeviceIdType.MESH


def dot(a, b, ca, cb):
    return lax.dot_general(a, b, (((ca,), (cb,)), ((), ())), preferred_element_type=F32)


def far_first(n):
    return sorted(range(1, n), key=lambda k: (-min(k, n - k), k))


def near_first(n):
    return sorted(range(1, n), key=lambda k: (min(k, n - k), k))


def kernel(
    x_ref, cot_ref, w_ref, out_ref, dx_ref, dw_ref,
    wq, wkv, accq, acckv, xall, xt, cots, outs, gq, gkv,
    sb, rb, pb, state, sc, rc, pc, suffix,
    part, q1, q1s, q2, q2s, k1, k1s, k2, k2s, v1, v1s, v2, v2s, last, fin,
    dxs, dxr, dxz, dxzr,
    load, aq_send, akv_send, aqy, aqx, akvy, akvx, x_send, x_recv, cot_send, cot_recv, out_send, out_recv,
    b_send, br, c_send, cr, d_send, dr, f_sem, dx_send, dx_recv,
):
    dp, seq = lax.axis_index("dp"), lax.axis_index("seq")
    z, core = dp // 2, dp % 2
    x, y = seq // NY, seq % NY
    zq = z % 2
    head = zq * 2 + core
    zmate = z + 1 - 2 * zq
    mate_dev = (zmate * 2 + core, seq)
    sib_dev = (z * 2 + 1 - core, seq)
    diag_dev = (zmate * 2 + 1 - core, seq)
    mate, sib, diag = (1 - zq) * 2 + core, zq * 2 + 1 - core, (1 - zq) * 2 + 1 - core
    pos = {"x": x, "y": y, "z": z}
    size = {"x": NX, "y": NY, "z": NZ}

    def at(axis, index):
        if axis == "x":
            return (dp, index * NY + y)
        if axis == "y":
            return (dp, x * NY + index)
        return (index * 2 + core, seq)

    def send(src, dst, s_sem, r_sem, device):
        pltpu.make_async_remote_copy(
            src_ref=src, dst_ref=dst, send_sem=s_sem, recv_sem=r_sem,
            device_id=device, device_id_type=MESH,
        ).start()

    def wait(ref, sem):
        pltpu.make_async_copy(ref, ref, sem).wait()

    def spread(axis, piece_for, landing, s_sem, r_sem):
        n, me = size[axis], pos[axis]
        for k in far_first(n):
            peer = (me + k) % n
            send(piece_for(peer), landing.at[me], s_sem, r_sem.at[k], at(axis, peer))

    def collect(axis, landing, r_sem):
        n, me = size[axis], pos[axis]
        for k in near_first(n):
            wait(landing.at[(me + n - k) % n], r_sem.at[k])

    loads = []
    for i in range(3):
        columns = pl.ds(pl.multiple_of(i * HD + head * DH, DH), DH)
        loads.append(
            pltpu.make_async_copy(
                w_ref.at[:, columns],
                wkv.at[seq, :, pl.ds((i - 1) * DH, DH)] if i else wq.at[seq],
                load.at[i],
            )
        )
    loads.append(pltpu.make_async_copy(x_ref, xall.at[head], load.at[3]))
    loads.append(
        pltpu.make_async_copy(
            cot_ref.at[:, pl.ds(pl.multiple_of(head * DH, DH), DH)], cots.at[head], load.at[4]
        )
    )
    for copy in loads:
        copy.start()

    barrier = pltpu.get_barrier_semaphore()
    peers = [sib_dev, diag_dev]
    peers += [(dp, (seq + k) % N_SEQ) for k in range(1, N_SEQ)]
    peers += [at("z", (z + k) % NZ) for k in range(1, NZ)]
    for device in peers:
        pl.semaphore_signal(barrier, inc=1, device_id=device, device_id_type=MESH)
    for copy in loads[:3]:
        copy.wait()
    pl.semaphore_wait(barrier, len(peers))

    key_value = (wkv, akv_send, akvy, akvx)
    queries = (wq, aq_send, aqy, aqx)

    def weights_to(group, index, axis, k):
        ref = group[0].at[index]
        send(ref, ref, group[1], group[3 if axis == "x" else 2].at[k], at(axis, (pos[axis] + k) % size[axis]))

    def weights_start(group):
        for k in near_first(NY):
            weights_to(group, seq, "y", k)
        for k in near_first(NX):
            weights_to(group, seq, "x", k)

    def weights_forward(group):
        for k in near_first(NY):
            index = x * NY + (y + NY - k) % NY
            wait(group[0].at[index], group[2].at[k])
            for kx in near_first(NX):
                weights_to(group, index, "x", kx)

    weights_start(key_value)
    halves = [pl.ds(i * (TOK // 2), TOK // 2) for i in range(2)]
    for i in range(2):
        send(x_ref.at[halves[i]], xall.at[head, halves[i]], x_send.at[0], x_recv.at[0, i], mate_dev)
    send(x_ref, xall.at[head], x_send.at[1], x_recv.at[1, 0], sib_dev)
    weights_start(queries)
    for i, (place, device) in enumerate(((mate, mate_dev), (diag, diag_dev), (sib, sib_dev))):
        columns = pl.ds(pl.multiple_of(place * DH, DH), DH)
        send(cot_ref.at[:, columns], cots.at[head], cot_send.at[i], cot_recv.at[i], device)
    weights_forward(key_value)
    for i in range(2):
        ref = xall.at[mate, halves[i]]
        wait(ref, x_recv.at[0, i])
        send(ref, ref, x_send.at[2], x_recv.at[2, i], sib_dev)
    weights_forward(queries)
    loads[3].wait()
    wait(xall.at[sib], x_recv.at[1, 0])
    for i in range(2):
        wait(xall.at[diag, halves[i]], x_recv.at[2, i])

    def project(group, total):
        for kx in (0, 1, 3, 2):
            xb = (x + NX - kx) % NX
            block = group[0].at[pl.ds(xb * NY, NY)]
            if kx:
                wait(block, group[3].at[kx])
            features = xall[:, :, pl.ds(pl.multiple_of(xb * 256, 256), 256)].reshape(QUAD * TOK, 256)
            term = dot(features, block[...].reshape(256, -1), 1, 0)
            if kx == 0:
                total[...] = term
            else:
                total[...] += term
        proj = total[...].astype(BF16)
        return [
            [proj[j * TOK : (j + 1) * TOK, i : i + DH] for j in range(QUAD)]
            for i in range(0, proj.shape[1], DH)
        ]

    key, value = project(key_value, acckv)
    rows_i = lax.broadcasted_iota(jnp.int32, (TOK, TOK), 0)
    cols_i = lax.broadcasted_iota(jnp.int32, (TOK, TOK), 1)
    causal = rows_i >= cols_i

    hops = sorted(
        ((kx, ky) for kx in range(NX) for ky in range(NY) if (kx, ky) != (0, 0)),
        key=lambda k: (-min(k[0], NX - k[0]) - min(k[1], NY - k[1]), k),
    )

    def exchange(src, landing, s_sem, r_sem):
        for kx, ky in hops:
            peer = (x + kx) % NX * NY + (y + ky) % NY
            send(src.at[peer], landing.at[seq], s_sem, r_sem, (dp, peer))
        landing[seq] = src[seq]

    def scan_start(local, s_buf, r_buf, s_sem, r_sem):
        for j in range(QUAD):
            s_buf[NY * j : NY * (j + 1)] = local[j].astype(BF16).reshape(NY, PIECE, DH)
        exchange(s_buf, r_buf, s_sem.at[0], r_sem.at[0])

    def scan_turn(r_buf, p_buf, landing, s_sem, r_sem, reverse):
        wait(r_buf.at[pl.ds(0, N_SEQ - 1)], r_sem.at[0])
        run = jnp.zeros((PIECE, DH), F32)
        for c in reversed(range(N_SEQ)) if reverse else range(N_SEQ):
            p_buf[c] = run.astype(BF16)
            run = run + r_buf[c].astype(F32)
        exchange(p_buf, landing, s_sem.at[1], r_sem.at[1])

    def scan_done(landing, r_sem):
        wait(landing.at[pl.ds(0, N_SEQ - 1)], r_sem.at[1])
        return [landing[NY * j : NY * (j + 1)].reshape(DH, DH) for j in range(QUAD)]

    scan_start([dot(key[j], value[j], 0, 0) for j in range(QUAD)], sb, rb, b_send, br)
    (query,) = project(queries, accq)
    scores = []
    mixed = []
    for j in range(QUAD):
        s = jnp.where(causal, dot(query[j], key[j], 1, 1), 0.0).astype(BF16)
        scores.append(s)
        mixed.append(dot(s, value[j], 1, 0))
    scan_turn(rb, pb, state, b_send, br, False)
    for j in range(QUAD):
        xt[:, j * TOK : (j + 1) * TOK] = xall[j].T
    loads[4].wait()
    for i, place in enumerate((mate, diag, sib)):
        wait(cots.at[place], cot_recv.at[i])
    states = scan_done(state, br)

    grad = []
    for j in range(QUAD):
        m = mixed[j] + dot(query[j], states[j], 1, 0)
        scale = lax.rsqrt(jnp.mean(m * m, axis=-1, keepdims=True) + EPS)
        o = m * scale
        outs[0, j] = o.astype(BF16)
        up = cots[j].astype(F32)
        grad.append((scale * (up - o * jnp.mean(up * o, axis=-1, keepdims=True))).astype(BF16))

    scan_start([dot(query[j], grad[j], 0, 0) for j in range(QUAD)], sc, rc, c_send, cr)
    for i, (place, device) in enumerate(((mate, mate_dev), (diag, diag_dev), (sib, sib_dev))):
        send(outs.at[0, place], outs.at[1, head], out_send.at[i], out_recv.at[i], device)
    outs[1, head] = outs[0, head]

    key_part, value_part = [], []
    for j in range(QUAD):
        back = jnp.where(causal, dot(grad[j], value[j], 1, 1), 0.0).astype(BF16)
        gq[j * TOK : (j + 1) * TOK, :] = (
            dot(back, key[j], 1, 0) + dot(grad[j], states[j], 1, 1)
        ).astype(BF16)
        key_part.append(dot(back, query[j], 0, 0))
        value_part.append(dot(scores[j], grad[j], 0, 0))

    def add_up(landing, start=0, step=1):
        total = landing[start].astype(F32)
        for c in range(start + step, landing.shape[0], step):
            total = total + landing[c].astype(F32)
        return total

    def first_x(group, landing):
        spread("x", lambda p: part.at[group, p], landing, d_send.at[group, 0], dr.at[group, 0])
        landing[x] = part[group, x]

    def first_y(group, landing):
        spread("y", lambda p: part.at[group, :, p], landing, d_send.at[group, 0], dr.at[group, 0])
        landing[y] = part[group, :, y]

    def second(group, axis_in, landing_in, mid, axis, landing):
        collect(axis_in, landing_in, dr.at[group, 0])
        mid[...] = add_up(landing_in).astype(BF16)
        spread(axis, lambda p: mid.at[p], landing, d_send.at[group, 1], dr.at[group, 1])
        landing[pos[axis]] = mid[pos[axis]]

    def third(group, axis_in, landing_in, mid):
        collect(axis_in, landing_in, dr.at[group, 1])
        mid[...] = add_up(landing_in).astype(BF16)
        spread("z", lambda p: mid, last.at[group], d_send.at[group, 2], dr.at[group, 2])
        last[group, z] = mid[...]

    def finish(group):
        collect("z", last.at[group], dr.at[group, 2])
        for way in range(2):
            fin[core, group, way] = add_up(last.at[group], way, 2)
        ref = fin.at[core, group]
        send(ref, ref, f_sem.at[0, group], f_sem.at[1, group], sib_dev)

    part[0] = dot(xt[...], gq[...], 1, 0).astype(BF16).reshape(NX, NY, ROWS, DH)
    scan_turn(rc, pc, suffix, c_send, cr, True)
    first_x(0, q1)
    suffixes = scan_done(suffix, cr)

    for j in range(QUAD):
        gkv[j * TOK : (j + 1) * TOK, 0:DH] = (
            key_part[j] + dot(value[j], suffixes[j], 1, 1)
        ).astype(BF16)
        gkv[j * TOK : (j + 1) * TOK, DH:] = (
            value_part[j] + dot(key[j], suffixes[j], 1, 0)
        ).astype(BF16)
    both = dot(xt[...], gkv[...], 1, 0).astype(BF16)
    part[2] = both[:, DH:].reshape(NX, NY, ROWS, DH)
    first_y(2, v1)
    part[1] = both[:, :DH].reshape(NX, NY, ROWS, DH)
    first_x(1, k1)
    second(0, "x", q1, q1s, "y", q2)

    def dx_term(j):
        start = pl.ds(pl.multiple_of(j * TOK, TOK), TOK)
        return dot(gq[start, :], wq[...].reshape(D, DH), 1, 1) + dot(
            gkv[start, :], wkv[...].reshape(D, 2 * DH), 1, 1
        )

    dxs[0] = dx_term(diag).astype(BF16)
    send(dxs.at[0], dxr.at[0], dx_send.at[0], dx_recv.at[0], sib_dev)
    dxs[1] = dx_term(sib).astype(BF16)
    send(dxs.at[1], dxr.at[1], dx_send.at[1], dx_recv.at[1], sib_dev)
    to_mate = dx_term(mate)
    wait(dxr.at[0], dx_recv.at[0])
    dxz[...] = (to_mate + dxr[0].astype(F32)).astype(BF16)
    send(dxz, dxzr, dx_send.at[2], dx_recv.at[2], mate_dev)

    second(1, "x", k1, k1s, "y", k2)
    second(2, "y", v1, v1s, "x", v2)
    third(0, "y", q2, q2s)
    third(1, "y", k2, k2s)
    third(2, "x", v2, v2s)

    own = dx_term(head)
    wait(dxr.at[1], dx_recv.at[1])
    wait(dxzr, dx_recv.at[2])
    dx_ref[...] = (own + dxr[1].astype(F32) + dxzr[...].astype(F32)).astype(BF16)
    for i, place in enumerate((mate, diag, sib)):
        wait(outs.at[1, place], out_recv.at[i])
    for h in range(HEADS):
        out_ref[:, h * DH : (h + 1) * DH] = outs[1, h]

    finish(0)
    finish(1)
    finish(2)
    for group in range(3):
        wait(fin.at[1 - core, group], f_sem.at[1, group])
        for h in range(HEADS):
            start = group * HD + h * DH
            dw_ref[:, start : start + DH] = fin[h % 2, group, h // 2]

    wait(wq.at[pl.ds(0, N_SEQ - 1)], aq_send)
    wait(wkv.at[pl.ds(0, N_SEQ - 1)], akv_send)
    for i in range(3):
        wait(xall.at[0], x_send.at[i])
        wait(cots.at[0], cot_send.at[i])
        wait(outs.at[0, 0], out_send.at[i])
        wait(dxz, dx_send.at[i])
    for s_sem in (b_send, c_send):
        wait(rb.at[pl.ds(0, N_SEQ - 1)], s_sem.at[0])
        wait(state.at[pl.ds(0, N_SEQ - 1)], s_sem.at[1])
    wait(q1.at[pl.ds(0, NX - 1)], d_send.at[0, 0])
    wait(q2.at[pl.ds(0, NY - 1)], d_send.at[0, 1])
    wait(k1.at[pl.ds(0, NX - 1)], d_send.at[1, 0])
    wait(k2.at[pl.ds(0, NY - 1)], d_send.at[1, 1])
    wait(v1.at[pl.ds(0, NY - 1)], d_send.at[2, 0])
    wait(v2.at[pl.ds(0, NX - 1)], d_send.at[2, 1])
    for group in range(3):
        wait(last.at[group, pl.ds(0, NZ - 1)], d_send.at[group, 2])
        wait(fin.at[0, group], f_sem.at[0, group])


def store(a_ref, b_ref, c_ref, a_out, b_out, c_out, sems):
    copies = [
        pltpu.make_async_copy(src, dst, sems.at[i])
        for i, (src, dst) in enumerate(((a_ref, a_out), (b_ref, b_out), (c_ref, c_out)))
    ]
    for copy in copies:
        copy.start()
    for copy in copies:
        copy.wait()


def shards(inputs, cotangent, qkv_weight):
    vmem = pl.BlockSpec(memory_space=pltpu.VMEM)
    hbm = pl.BlockSpec(memory_space=pltpu.HBM)
    dma = pltpu.SemaphoreType.DMA
    scan_bufs = [
        pltpu.VMEM((N_SEQ, PIECE, DH), BF16),
        pltpu.VMEM((N_SEQ, PIECE, DH), BF16),
        pltpu.VMEM((N_SEQ, PIECE, DH), BF16),
        pltpu.VMEM((N_SEQ, PIECE, DH), BF16),
    ]
    x_bufs = [
        pltpu.VMEM((NX, NY, ROWS, DH), BF16),
        pltpu.VMEM((NY, ROWS, DH), BF16),
        pltpu.VMEM((NY, ROWS, DH), BF16),
        pltpu.VMEM((ROWS, DH), BF16),
    ]
    y_bufs = [
        pltpu.VMEM((NY, NX, ROWS, DH), BF16),
        pltpu.VMEM((NX, ROWS, DH), BF16),
        pltpu.VMEM((NX, ROWS, DH), BF16),
        pltpu.VMEM((ROWS, DH), BF16),
    ]
    out, dx, dw = pl.pallas_call(
        kernel,
        name="layer",
        out_shape=(
            jax.ShapeDtypeStruct((TOK, HD), BF16),
            jax.ShapeDtypeStruct((TOK, D), BF16),
            jax.ShapeDtypeStruct((ROWS, 3 * HD), F32),
        ),
        in_specs=[hbm] * 3,
        out_specs=(vmem,) * 3,
        scratch_shapes=[
            pltpu.VMEM((N_SEQ, ROWS, DH), BF16),
            pltpu.VMEM((N_SEQ, ROWS, 2 * DH), BF16),
            pltpu.VMEM((QUAD * TOK, DH), F32),
            pltpu.VMEM((QUAD * TOK, 2 * DH), F32),
            pltpu.VMEM((QUAD, TOK, D), BF16),
            pltpu.VMEM((D, QUAD * TOK), BF16),
            pltpu.VMEM((QUAD, TOK, DH), BF16),
            pltpu.VMEM((2, QUAD, TOK, DH), BF16),
            pltpu.VMEM((QUAD * TOK, DH), BF16),
            pltpu.VMEM((QUAD * TOK, 2 * DH), BF16),
            *scan_bufs,
            *scan_bufs,
            pltpu.VMEM((3, NX, NY, ROWS, DH), BF16),
            *x_bufs,
            *x_bufs,
            *y_bufs,
            pltpu.VMEM((3, NZ, ROWS, DH), BF16),
            pltpu.VMEM((2, 3, 2, ROWS, DH), F32),
            pltpu.VMEM((2, TOK, D), BF16),
            pltpu.VMEM((2, TOK, D), BF16),
            pltpu.VMEM((TOK, D), BF16),
            pltpu.VMEM((TOK, D), BF16),
            dma((5,)),
            dma(()),
            dma(()),
            dma((NY,)),
            dma((NX,)),
            dma((NY,)),
            dma((NX,)),
            dma((3,)),
            dma((3, 2)),
            dma((3,)),
            dma((3,)),
            dma((3,)),
            dma((3,)),
            dma((2,)),
            dma((2,)),
            dma((2,)),
            dma((2,)),
            dma((3, 3)),
            dma((3, 3, NY)),
            dma((2, 3)),
            dma((3,)),
            dma((3,)),
        ],
        compiler_params=pltpu.CompilerParams(
            collective_id=0, has_side_effects=True, vmem_limit_bytes=40 * 1024 * 1024
        ),
    )(*(pltpu.with_memory_space_constraint(a, pltpu.HBM) for a in (inputs[0], cotangent[0], qkv_weight)))
    out, dx, dw = pl.pallas_call(
        store,
        name="store",
        out_shape=(
            jax.ShapeDtypeStruct((TOK, HD), BF16),
            jax.ShapeDtypeStruct((TOK, D), BF16),
            jax.ShapeDtypeStruct((ROWS, 3 * HD), F32),
        ),
        in_specs=[vmem] * 3,
        out_specs=(hbm,) * 3,
        scratch_shapes=[dma((3,))],
        compiler_params=pltpu.CompilerParams(vmem_limit_bytes=4 * 1024 * 1024),
    )(out, dx, dw)
    return out[None], dx[None], dw


def solution(mesh):
    in_specs = (P("dp", "seq", None), P("dp", "seq", None), P("seq", None))
    out_specs = (P("dp", "seq", None), P("dp", "seq", None), P("seq", None))
    return jax.shard_map(shards, mesh=mesh, in_specs=in_specs, out_specs=out_specs, check_vma=False)
```
